32 devices in a mesh: dp: 4 (over y, x), seq: 2 (over core), tensor: 4 (over z).
Axes of the slice: x: 2, y: 2, z: 4, core: 2. Of those that a mesh axis runs over, the one named last changes fastest.
Arguments:
- x_in: bfloat16 [4, 1024, 8192], P('dp', 'seq', 'tensor'), may hold values from -0.0625 to 0.0625
- b_in: bfloat16 [4, 1024, 1024], P('dp', 'seq', 'tensor'), may hold values from -3 to 3
- c_in: bfloat16 [4, 1024, 1024], P('dp', 'seq', 'tensor'), may hold values from -3 to 3
- log_decay: float32 [4, 1024, 128], P('dp', 'seq', 'tensor'), may hold values from -1 to 0, as said below
- out_weight: bfloat16 [8192, 4096], P('tensor'), may hold values from -0.0625 to 0.0625
- out_grad: bfloat16 [4, 1024, 4096], P('dp', 'seq', 'tensor'), may hold values from -0.078125 to 0.078125
Outputs:
- weight_grad: bfloat16 [8192, 4096], P('tensor', ('dp', 'seq'))
- x_grad: bfloat16 [4, 1024, 8192], P('dp', 'seq', 'tensor')
- b_grad: bfloat16 [4, 1024, 1024], P('dp', 'seq', 'tensor')
- c_grad: bfloat16 [4, 1024, 1024], P('dp', 'seq', 'tensor')
The draws below stay inside these ranges and needn't reach their ends.
Inputs may be any that keep to these rules, and one draw needn't show every extreme that they name: `log_decay`: every log-decay is below zero.
All inputs are finite; a program needn't handle non-finite values.
Results may differ from the reference program's by a relative error of at most 0.017.
Values may be sent and summed in bfloat16 or wider, within the bound.
No kernel may reach another device: no remote copies, remote signals or barrier semaphores. Data moves between devices by JAX's collectives and lax.ppermute only.
A program may use at most 192 MiB of HBM per device.

```python
import math
import jax
import jax.numpy as jnp
from jax import lax

WIDTH = 4096
HEADS = 128
HEAD_DIM = 64
STATE = 128
GROUPS = 8
SPAN = 256
INNER = 8192
REPO_COUNT = 4
REPO_TOKENS = 1024


def draw_log_decay(key, part):
    split_keys = jax.random.split(key, 7)
    keep_tenths = 5
    is_slow = jax.random.randint(split_keys[0], (HEADS,), 0, 10) < keep_tenths
    slow_rate = math.log(10.0) / REPO_TOKENS * jax.random.uniform(split_keys[1], (HEADS,), minval=0.1, maxval=0.4)
    fast_rate = jnp.exp(jax.random.uniform(split_keys[2], (HEADS,), minval=math.log(1.0 / 50.0), maxval=math.log(1.0 / 20.0)))
    decay_factors = jnp.where(is_slow, slow_rate, fast_rate)
    block_list = jnp.exp(jax.random.uniform(split_keys[3], (REPO_COUNT, REPO_TOKENS // SPAN, HEADS), minval=math.log(0.5), maxval=math.log(2.0)))
    block_list = jnp.repeat(block_list, SPAN, axis=1)
    jitter_level = jax.random.uniform(split_keys[4], (REPO_COUNT, REPO_TOKENS, HEADS), minval=0.3, maxval=1.7)
    spike_positions = jax.random.randint(split_keys[5], (REPO_COUNT, 2), 0, REPO_TOKENS)
    loss_values = jax.random.uniform(split_keys[6], (REPO_COUNT, 2, HEADS), minval=0.2, maxval=0.4)
    at_position = (jnp.arange(REPO_TOKENS)[None, :, None] == spike_positions[:, None, :]).astype(jnp.float32)
    spike_values = jnp.sum(at_position[..., None] * (-jnp.log(1.0 - loss_values))[:, None], axis=2)
    return -(decay_factors * block_list * jitter_level + spike_values)


def strengthened(drawn, stream_key, source, target, shards_of, factor):
    def block_of(axis_at):
        return (jnp.arange(drawn.shape[axis_at]) // (drawn.shape[axis_at] // shards_of)).reshape((-1,) + (1,) * (drawn.ndim - 1 - axis_at))

    first = jax.random.permutation(stream_key, shards_of)[block_of(target)]
    other_side = (block_of(target) + shards_of // 2) % shards_of
    return jnp.where((block_of(source) == first) | (block_of(source) == other_side), factor * drawn, drawn)


def shard_levels(own_key, extent, cuts, smallest, largest):
    loudness = 1.0
    for axis_at, shards_of in cuts:
        heights = jax.random.uniform(jax.random.fold_in(jax.random.fold_in(own_key, 6), axis_at), (shards_of,), jnp.float32, smallest / len(cuts), largest / len(cuts))
        loudness = loudness * jnp.repeat(jnp.exp(heights), extent[axis_at] // shards_of).reshape((-1,) + (1,) * (len(extent) - 1 - axis_at))
    return loudness


def normal_values(key, dims, scale, limit, cuts=(), dtype=jnp.bfloat16):
    array = scale * jax.random.normal(key, dims, jnp.float32)
    if cuts:
        array = array * shard_levels(key, dims, cuts, -0.22, 0.18)
    return jnp.clip(array, -limit, limit).astype(dtype)


def noise_with(own_key, dims, scale, reach, cuts, heavy, kind=jnp.bfloat16):
    values = scale * jax.random.normal(own_key, dims, jnp.float32)
    if cuts:
        values = values * shard_levels(own_key, dims, cuts, -0.22, 0.18)
    return jnp.clip(strengthened(values, jax.random.fold_in(own_key, 3), *heavy), -reach, reach).astype(kind)


def setup_inputs(seed: int = 0) -> dict:
    keys = jax.random.split(jax.random.key(seed), 7)
    x_in = normal_values(keys[0], (REPO_COUNT, REPO_TOKENS, INNER), 0.01, 0.0625, ((0, 4), (1, 2), (2, 4)))
    b_in = normal_values(keys[1], (REPO_COUNT, REPO_TOKENS, GROUPS * STATE), 0.5, 3.0, ((0, 4), (1, 2), (2, 4)))
    c_in = normal_values(keys[2], (REPO_COUNT, REPO_TOKENS, GROUPS * STATE), 0.5, 3.0, ((0, 4), (1, 2), (2, 4)))
    log_decay = draw_log_decay(jax.random.fold_in(keys[6], 71), 0)
    out_weight = normal_values(keys[4], (INNER, WIDTH), INNER ** -0.5, 0.0625, ((0, 4),))
    out_grad = noise_with(keys[5], (REPO_COUNT, REPO_TOKENS, WIDTH), 0.01, 0.078125, ((0, 4), (1, 2), (2, 4)), (1, 2, 4, 2.0))
    return dict(x_in=x_in, b_in=b_in, c_in=c_in, log_decay=log_decay, out_weight=out_weight, out_grad=out_grad)


highest = lax.Precision.HIGHEST

def decay_terms(decays):
    running = jnp.cumsum(decays, axis=1)
    totals = running[:, -1]
    by_head = jnp.transpose(running, (0, 2, 3, 1))
    spread = by_head[..., :, None] - by_head[..., None, :]
    places = jnp.arange(decays.shape[1])
    causal = places[:, None] >= places[None, :]
    within = jnp.where(causal, jnp.exp(jnp.minimum(spread, 0.0)), 0.0)
    to_end = jnp.exp(totals[:, None] - running)
    from_start = jnp.exp(running)
    return (totals, within, to_end, from_start)

def forward_states(totals, span_adds):

    def advance(carried, inputs):
        return (jnp.exp(inputs[0])[..., None, None] * carried + inputs[1], carried)
    last_state, entering = lax.scan(advance, jnp.zeros_like(span_adds[0]), (totals, span_adds))
    return (entering, last_state)

def item_forward(values, writes, read_rows, decays):
    totals, within, to_end, from_start = decay_terms(decays)
    affinity = jnp.einsum('cign,cjgn->cgij', read_rows, writes, precision=highest)
    weights = affinity[:, :, None] * within
    inner_out = jnp.einsum('cgrij,cjgrp->cigrp', weights, values, precision=highest)
    span_adds = jnp.einsum('cjgn,cjgrp->cgrnp', writes, to_end[..., None] * values, precision=highest)
    entering, last_state = forward_states(totals, span_adds)
    carried_out = jnp.einsum('cign,cgrnp->cigrp', read_rows, entering, precision=highest)
    return inner_out + carried_out * from_start[..., None]

def reference(x_in, b_in, c_in, log_decay, out_weight, out_grad):
    per_group = HEADS // GROUPS
    spans = REPO_TOKENS // SPAN
    item_count = REPO_COUNT * GROUPS
    y_grad = jnp.dot(out_grad.reshape(REPO_COUNT * REPO_TOKENS, WIDTH), out_weight.T, preferred_element_type=jnp.float32).astype(jnp.bfloat16)

    def heads_first(source):
        shaped = source.astype(jnp.float32).reshape(REPO_COUNT, REPO_TOKENS, GROUPS, per_group, HEAD_DIM)
        return shaped.transpose(0, 2, 1, 3, 4).reshape(item_count, spans, SPAN, 1, per_group, HEAD_DIM)

    def groups_first(source):
        shaped = source.astype(jnp.float32).reshape(REPO_COUNT, REPO_TOKENS, GROUPS, STATE)
        return shaped.transpose(0, 2, 1, 3).reshape(item_count, spans, SPAN, 1, STATE)
    decays = log_decay.reshape(REPO_COUNT, REPO_TOKENS, GROUPS, per_group).transpose(0, 2, 1, 3)
    decays = decays.reshape(item_count, spans, SPAN, 1, per_group)

    def per_item(inputs):
        values, writes, read_rows, decay_item, grad_item = inputs
        outputs, pullback = jax.vjp(lambda value_arg, write_arg, read_arg: item_forward(value_arg, write_arg, read_arg, decay_item), values, writes, read_rows)
        gradients = pullback(grad_item)
        return (outputs, gradients[0], gradients[1], gradients[2])
    scan_out, x_part, b_part, c_part = lax.map(per_item, (heads_first(x_in), groups_first(b_in), groups_first(c_in), decays, heads_first(y_grad.reshape(REPO_COUNT, REPO_TOKENS, INNER))))

    def heads_back(source):
        return source.reshape(REPO_COUNT, GROUPS, REPO_TOKENS, per_group * HEAD_DIM).transpose(0, 2, 1, 3).reshape(REPO_COUNT, REPO_TOKENS, INNER)

    def groups_back(source):
        return source.reshape(REPO_COUNT, GROUPS, REPO_TOKENS, STATE).transpose(0, 2, 1, 3).reshape(REPO_COUNT, REPO_TOKENS, GROUPS * STATE)
    scan_rows = heads_back(scan_out).astype(jnp.bfloat16)
    weight_grad = jnp.dot(scan_rows.reshape(REPO_COUNT * REPO_TOKENS, INNER).T, out_grad.reshape(REPO_COUNT * REPO_TOKENS, WIDTH), preferred_element_type=jnp.float32).astype(jnp.bfloat16)
    return (weight_grad, heads_back(x_part).astype(jnp.bfloat16), groups_back(b_part).astype(jnp.bfloat16), groups_back(c_part).astype(jnp.bfloat16))
```

```python
import functools

import jax
import jax.numpy as jnp
from jax import lax
from jax.experimental import pallas as pl
from jax.experimental.pallas import tpu as pltpu
from jax.sharding import PartitionSpec as P

HEAD_DIM = 64
STATE = 128
CHUNK = 128
LANES = 128
PARTS = 1

BF16 = jnp.bfloat16
F32 = jnp.float32


def dot(a, b, dims):
    return lax.dot_general(a, b, (dims, ((), ())), preferred_element_type=F32)


NN = ((1,), (0,))
NT = ((1,), (1,))
TN = ((0,), (0,))


def causal_mask():
    rows = lax.broadcasted_iota(jnp.int32, (CHUNK, CHUNK), 0)
    cols = lax.broadcasted_iota(jnp.int32, (CHUNK, CHUNK), 1)
    return rows >= cols


def chunk_decays(decays):
    ones = jnp.where(causal_mask(), 1.0, 0.0).astype(BF16)
    first = decays.astype(BF16)
    rest = decays - first.astype(F32)
    second = rest.astype(BF16)
    third = (rest - second.astype(F32)).astype(BF16)
    running = dot(ones, first, NN) + dot(ones, second, NN) + dot(ones, third, NN)
    half = 0.5 * running[CHUNK - 1 : CHUNK, :]
    return jnp.exp(running - half), jnp.exp(half - running), jnp.exp(half)


def over_columns(factors, block):
    rows = factors.shape[0]
    per_block = LANES // HEAD_DIM
    lanes = lax.broadcasted_iota(jnp.int32, (rows, LANES), 1)
    head = block * per_block
    return jnp.where(
        lanes < HEAD_DIM,
        jnp.broadcast_to(factors[:, head : head + 1], (rows, LANES)),
        jnp.broadcast_to(factors[:, head + 1 : head + 2], (rows, LANES)),
    )


def over_group(factors, group, width):
    blocks = width // LANES
    return jnp.concatenate(
        [over_columns(factors, group * blocks + i) for i in range(blocks)], axis=1
    )


def states_kernel(x_ref, b_ref, decay_ref, scaled_ref, state_ref, *, groups):
    chunk = pl.program_id(0)
    width = x_ref.shape[1] // groups

    @pl.when(chunk == 0)
    def _():
        state_ref[...] = jnp.zeros_like(state_ref)

    _, shrink, half = chunk_decays(decay_ref[...])
    for g in range(groups):
        cols = slice(g * width, (g + 1) * width)
        scaled = (x_ref[:, cols].astype(F32) * over_group(shrink, g, width)).astype(BF16)
        scaled_ref[:, cols] = scaled
        writes = b_ref[:, g * STATE : (g + 1) * STATE]
        halves = over_group(half, g, width)
        rows = slice(g * STATE, (g + 1) * STATE)
        state_ref[rows, :] = halves * (halves * state_ref[rows, :] + dot(writes, scaled, TN))


def scan_kernel(
    scaled_ref, b_ref, c_ref, decay_ref, enter_ref, rows_ref, held_ref, state_ref, *, groups
):
    chunk = pl.program_id(0)
    width = scaled_ref.shape[1] // groups

    @pl.when(chunk == 0)
    def _():
        state_ref[...] = enter_ref[...]

    grow, _, half = chunk_decays(decay_ref[...])
    mask = causal_mask()
    for g in range(groups):
        cols = slice(g * width, (g + 1) * width)
        rows = slice(g * STATE, (g + 1) * STATE)
        scaled = scaled_ref[:, cols]
        writes = b_ref[:, rows]
        reads = c_ref[:, rows]
        halves = over_group(half, g, width)
        held = halves * state_ref[rows, :]
        held_low = held.astype(BF16)
        held_ref[0, rows, :] = held_low
        affinity = jnp.where(mask, dot(reads, writes, NT), 0.0).astype(BF16)
        out = dot(affinity, scaled, NN) + dot(reads, held_low, NN)
        out = out * over_group(grow, g, width)
        rows_ref[cols, :] = out.T.astype(BF16)
        state_ref[rows, :] = halves * (held + dot(writes, scaled, TN))


def pulls_kernel(grad_ref, c_ref, decay_ref, scaled_ref, state_ref, *, groups):
    step = pl.program_id(0)
    width = grad_ref.shape[1] // groups

    @pl.when(step == 0)
    def _():
        state_ref[...] = jnp.zeros_like(state_ref)

    grow, _, half = chunk_decays(decay_ref[...])
    for g in range(groups):
        cols = slice(g * width, (g + 1) * width)
        rows = slice(g * STATE, (g + 1) * STATE)
        scaled = (grad_ref[:, cols].astype(F32) * over_group(grow, g, width)).astype(BF16)
        scaled_ref[:, cols] = scaled
        halves = over_group(half, g, width)
        pulled = dot(c_ref[:, rows], scaled, TN)
        state_ref[rows, :] = halves * (halves * state_ref[rows, :] + pulled)


def grads_kernel(
    grad_ref, scaled_ref, b_ref, c_ref, decay_ref, held_ref, leave_ref,
    x_grad_ref, b_grad_ref, c_grad_ref, state_ref, *, groups,
):
    step = pl.program_id(0)
    width = grad_ref.shape[1] // groups

    @pl.when(step == 0)
    def _():
        state_ref[...] = leave_ref[...]

    _, shrink, half = chunk_decays(decay_ref[...])
    mask = causal_mask()
    for g in range(groups):
        cols = slice(g * width, (g + 1) * width)
        rows = slice(g * STATE, (g + 1) * STATE)
        grad = grad_ref[:, cols]
        scaled = scaled_ref[:, cols]
        writes = b_ref[:, rows]
        reads = c_ref[:, rows]
        halves = over_group(half, g, width)
        left = halves * state_ref[rows, :]
        left_low = left.astype(BF16)
        affinity = jnp.where(mask, dot(reads, writes, NT), 0.0).astype(BF16)
        x_grad = dot(affinity, grad, TN) + dot(writes, left_low, NN)
        x_grad_ref[:, cols] = (x_grad * over_group(shrink, g, width)).astype(BF16)
        pair = jnp.where(mask, dot(grad, scaled, NT), 0.0).astype(BF16)
        c_grad = dot(pair, writes, NN) + dot(grad, held_ref[0, rows, :], NT)
        c_grad_ref[:, rows] = c_grad.astype(BF16)
        b_grad = dot(pair, reads, TN) + dot(scaled, left_low, NT)
        b_grad_ref[:, rows] = b_grad.astype(BF16)
        state_ref[rows, :] = halves * (left + dot(reads, grad, TN))


def scan_calls(tokens, heads, groups):
    inner = heads * HEAD_DIM
    width = inner // groups
    keys = groups * STATE
    chunks = tokens // CHUNK
    call = functools.partial(pl.pallas_call, grid=(chunks,))

    def ahead(cols):
        return pl.BlockSpec((CHUNK, cols), lambda i: (i, 0))

    def back(cols):
        return pl.BlockSpec((CHUNK, cols), lambda i: (chunks - 1 - i, 0))

    whole = pl.BlockSpec((keys, width), lambda i: (0, 0))
    state_type = jax.ShapeDtypeStruct((keys, width), F32)
    rows_type = jax.ShapeDtypeStruct((tokens, inner), BF16)
    keys_type = jax.ShapeDtypeStruct((tokens, keys), BF16)
    held_type = jax.ShapeDtypeStruct((chunks, keys, width), BF16)
    scratch = [pltpu.VMEM((keys, width), F32)]
    states = call(
        functools.partial(states_kernel, groups=groups),
        in_specs=[ahead(inner), ahead(keys), ahead(heads)],
        out_specs=[ahead(inner), whole],
        out_shape=[rows_type, state_type],
        name="states",
    )
    scan = call(
        functools.partial(scan_kernel, groups=groups),
        in_specs=[ahead(inner), ahead(keys), ahead(keys), ahead(heads), whole],
        out_specs=[
            pl.BlockSpec((inner, CHUNK), lambda i: (0, i)),
            pl.BlockSpec((1, keys, width), lambda i: (i, 0, 0)),
        ],
        out_shape=[jax.ShapeDtypeStruct((inner, tokens), BF16), held_type],
        scratch_shapes=scratch,
        name="scan",
    )
    pulls = call(
        functools.partial(pulls_kernel, groups=groups),
        in_specs=[back(inner), back(keys), back(heads)],
        out_specs=[back(inner), whole],
        out_shape=[rows_type, state_type],
        name="pulls",
    )
    grads = call(
        functools.partial(grads_kernel, groups=groups),
        in_specs=[
            back(inner), back(inner), back(keys), back(keys), back(heads),
            pl.BlockSpec((1, keys, width), lambda i: (chunks - 1 - i, 0, 0)), whole,
        ],
        out_specs=[back(inner), back(keys), back(keys)],
        out_shape=[rows_type, keys_type, keys_type],
        scratch_shapes=scratch,
        name="grads",
    )
    return states, scan, pulls, grads


def passed_along(shard, axis, by):
    length = lax.axis_size(axis)
    pairs = [(i, i + by) for i in range(length) if 0 <= i + by < length]
    return lax.ppermute(shard, axis, pairs)


def chained(local, log_decay, groups, axis, by):
    incoming = passed_along(local, axis, by)
    turns = lax.axis_size(axis) - 1
    if turns > 1:
        total = jnp.exp(jnp.sum(log_decay, axis=0)).reshape(groups, 1, -1)
        spread = jnp.repeat(total, HEAD_DIM, axis=2)
        spread = jnp.broadcast_to(spread, (groups, STATE, spread.shape[2]))
        spread = spread.reshape(local.shape)

        def turn(_, arrived):
            return passed_along(spread * arrived + local, axis, by)

        incoming = lax.fori_loop(0, turns - 1, turn, incoming)
    return incoming


def any_mesh(rows_t, out_grad, out_weight):
    full = lax.all_gather(out_grad, "tensor", axis=1, tiled=True)
    y_grad = lax.dot_general(
        full, out_weight, (NT, ((), ())), preferred_element_type=F32
    ).astype(BF16)
    part = lax.dot_general(rows_t, full, (NN, ((), ())), preferred_element_type=F32)
    weight_grad = lax.psum_scatter(
        part.astype(BF16), ("dp", "seq"), scatter_dimension=1, tiled=True
    )
    return y_grad, weight_grad


def project_kernel(table_ref, slots_ref, low_ref, high_ref, *refs, first, last):
    step = pl.program_id(0)
    out_ref, total_ref = refs[-2:]
    got = dot(slots_ref[0, 0], low_ref[...], NT) + dot(slots_ref[0, 1], high_ref[...], NT)

    @pl.when(step == 0)
    def _():
        total_ref[...] = got if first else refs[0][...] + got

    @pl.when(step > 0)
    def _():
        total_ref[...] += got

    @pl.when(step == pl.num_programs(0) - 1)
    def _():
        out_ref[...] = total_ref[...].astype(out_ref.dtype)


def project(table, slots, out_weight, part, parts, before):
    tokens, wide = slots.shape[2:]
    inner = out_weight.shape[0]
    first, last = before is None, part == parts - 1
    whole = pl.BlockSpec((tokens, inner), lambda i, t: (0, 0))
    return pl.pallas_call(
        functools.partial(project_kernel, first=first, last=last),
        grid_spec=pltpu.PrefetchScalarGridSpec(
            num_scalar_prefetch=1,
            grid=(4,),
            in_specs=[
                pl.BlockSpec((1, 2, tokens, wide), lambda i, t: (i, 0, 0, 0)),
                pl.BlockSpec((inner, wide), lambda i, t: (0, t[4 + i] * 2 * parts + part)),
                pl.BlockSpec((inner, wide), lambda i, t: (0, (t[4 + i] * 2 + 1) * parts + part)),
            ]
            + ([] if first else [whole]),
            out_specs=whole,
            scratch_shapes=[pltpu.VMEM((tokens, inner), F32)],
        ),
        out_shape=jax.ShapeDtypeStruct((tokens, inner), BF16 if last else F32),
        name="project",
    )(table, slots, out_weight, out_weight, *([] if first else [before]))


def partial_kernel(table_ref, own_ref, other_ref, mine_ref, theirs_ref, x_ref, y_ref):
    step = pl.program_id(0)
    got = dot(own_ref[...], mine_ref[0, 0], NN) + dot(other_ref[...], theirs_ref[0], NN)
    got = got.astype(BF16)

    @pl.when(step < 2)
    def _():
        x_ref[0] = got

    @pl.when(step >= 2)
    def _():
        y_ref[0] = got


def partials(table, own, other, slots, theirs, targets, name):
    inner, tokens = own.shape
    half = inner // 2
    wide = slots.shape[3]

    def slot(i, t):
        picked = t[targets[3]]
        for place in (2, 1, 0):
            picked = jnp.where(i == place, t[targets[place]], picked)
        return picked

    rows = pl.BlockSpec((half, tokens), lambda i, t: (i // 2, 0))
    out_type = jax.ShapeDtypeStruct((2, half, wide), BF16)
    return pl.pallas_call(
        partial_kernel,
        grid_spec=pltpu.PrefetchScalarGridSpec(
            num_scalar_prefetch=1,
            grid=(4,),
            in_specs=[
                rows,
                rows,
                pl.BlockSpec((1, 1, tokens, wide), lambda i, t: (slot(i, t), t[8], 0, 0)),
                pl.BlockSpec((1, tokens, wide), lambda i, t: (slot(i, t), 0, 0)),
            ],
            out_specs=[
                pl.BlockSpec((1, half, wide), lambda i, t: (jnp.minimum(i, 1), 0, 0)),
                pl.BlockSpec((1, half, wide), lambda i, t: (jnp.maximum(i - 2, 0), 0, 0)),
            ],
        ),
        out_shape=[out_type, out_type],
        name=name,
    )(table, own, other, slots, theirs)


def swapped(value, axis, by):
    return lax.ppermute(value, axis, [(i, i ^ by) for i in range(lax.axis_size(axis))])


def total(*terms):
    return functools.reduce(jnp.add, [t.astype(F32) for t in terms]).astype(BF16)


def gathered(own, place, after):
    own = own if after is None else lax.optimization_barrier((own, after))[0]
    up = passed_along(own, "tensor", 1)
    down = passed_along(own, "tensor", -1)
    across = swapped_across(own)
    far = lax.ppermute(across, "tensor", [(1, 0), (2, 3)])
    slots = jnp.stack(
        [own, jnp.where(place == 0, far, up), across, jnp.where(place == 3, far, down)]
    )
    return slots, across


def swapped_across(own):
    return lax.ppermute(own, "tensor", [(i, (i + 2) % 4) for i in range(4)])


def this_mesh(rows_t, out_grad, out_weight):
    tokens, features = out_grad.shape
    parts = PARTS
    wide = features // 2 // parts
    place = lax.axis_index("tensor")
    repo = lax.axis_index("dp")
    core = lax.axis_index("seq")
    table = jnp.stack(
        [(place - (repo ^ r)) % 4 for r in range(4)]
        + [(place - s) % 4 for s in range(4)]
        + [core]
    ).astype(jnp.int32)
    split = out_grad.reshape(tokens, 2, parts, wide).transpose(2, 1, 0, 3)
    other = swapped(rows_t, "seq", 1)
    y_grad = None
    after = None
    pieces = []
    for part in range(parts):
        slots, after = gathered(split[part], place, after)
        theirs = lax.dynamic_index_in_dim(slots, 1 - core, 1, keepdims=False)
        theirs = swapped(theirs, "seq", 1)
        x_send, y_send = partials(table, rows_t, other, slots, theirs, (1, 3, 2, 3), "sent")
        x_got = swapped(x_send, "dp", 1)
        y_got = swapped(y_send, "dp", 2)
        x_kept, y_kept = partials(table, rows_t, other, slots, theirs, (0, 2, 0, 1), "kept")
        x_last = swapped(total(x_kept[1], x_got[1]), "dp", 2)
        y_last = swapped(total(y_kept[1], y_got[1]), "dp", 1)
        pieces.append(
            jnp.concatenate(
                [total(x_kept[0], x_got[0], x_last), total(y_kept[0], y_got[0], y_last)]
            )
        )
        y_grad = project(table, slots, out_weight, part, parts, y_grad)
    return y_grad, jnp.concatenate(pieces, axis=1)


def per_device(x_in, b_in, c_in, log_decay, out_weight, out_grad):
    x_in, b_in, c_in, log_decay, out_grad = (
        x_in[0], b_in[0], c_in[0], log_decay[0], out_grad[0],
    )
    tokens, heads = log_decay.shape
    groups = b_in.shape[1] // STATE
    states, scan, pulls, grads = scan_calls(tokens, heads, groups)
    scaled, end_local = states(x_in, b_in, log_decay)
    entering = chained(end_local, log_decay, groups, "seq", 1)
    rows_t, held = scan(scaled, b_in, c_in, log_decay, entering)
    sizes = tuple(lax.axis_size(name) for name in ("dp", "seq", "tensor"))
    project_both = this_mesh if sizes == (4, 2, 4) else any_mesh
    y_grad, weight_grad = project_both(rows_t, out_grad, out_weight)
    grad, start_local = pulls(y_grad, c_in, log_decay)
    leaving = chained(start_local, log_decay, groups, "seq", -1)
    x_grad, b_grad, c_grad = grads(grad, scaled, b_in, c_in, log_decay, held, leaving)
    return weight_grad, x_grad[None], b_grad[None], c_grad[None]


def solution(mesh):
    tokens_spec = P("dp", "seq", "tensor")
    return jax.shard_map(
        per_device,
        mesh=mesh,
        in_specs=(tokens_spec,) * 4 + (P("tensor", None), tokens_spec),
        out_specs=(P("tensor", ("dp", "seq")),) + (tokens_spec,) * 3,
        check_vma=False,
    )
```

```python
import functools

import jax
import jax.numpy as jnp
from jax import lax
from jax.experimental import pallas as pl
from jax.experimental.pallas import tpu as pltpu
from jax.sharding import PartitionSpec as P


HEAD_DIM = 64
STATE = 128
CHUNK = 128
LANES = 128
PARTS = 2
THIS_MESH = (4, 2, 4)

BF16 = jnp.bfloat16
F32 = jnp.float32


def dot(a, b, dims):
    return lax.dot_general(a, b, (dims, ((), ())), preferred_element_type=F32)


NN = ((1,), (0,))
NT = ((1,), (1,))
TN = ((0,), (0,))


def causal_mask():
    rows = lax.broadcasted_iota(jnp.int32, (CHUNK, CHUNK), 0)
    cols = lax.broadcasted_iota(jnp.int32, (CHUNK, CHUNK), 1)
    return rows >= cols


def chunk_decays(decays):
    ones = jnp.where(causal_mask(), 1.0, 0.0).astype(BF16)
    first = decays.astype(BF16)
    rest = decays - first.astype(F32)
    second = rest.astype(BF16)
    third = (rest - second.astype(F32)).astype(BF16)
    running = dot(ones, first, NT) + dot(ones, second, NT) + dot(ones, third, NT)
    half = 0.5 * running[CHUNK - 1 : CHUNK, :]
    return jnp.exp(running - half), jnp.exp(half - running), jnp.exp(half)


def over_columns(factors, block):
    rows = factors.shape[0]
    per_block = LANES // HEAD_DIM
    lanes = lax.broadcasted_iota(jnp.int32, (rows, LANES), 1)
    head = block * per_block
    return jnp.where(
        lanes < HEAD_DIM,
        jnp.broadcast_to(factors[:, head : head + 1], (rows, LANES)),
        jnp.broadcast_to(factors[:, head + 1 : head + 2], (rows, LANES)),
    )


def over_group(factors, group, width):
    blocks = width // LANES
    return jnp.concatenate(
        [over_columns(factors, group * blocks + i) for i in range(blocks)], axis=1
    )


def states_kernel(x_ref, b_ref, decay_ref, scaled_ref, state_ref, *, groups):
    chunk = pl.program_id(0)
    width = x_ref.shape[1] // groups

    @pl.when(chunk == 0)
    def _():
        state_ref[...] = jnp.zeros_like(state_ref)

    _, shrink, half = chunk_decays(decay_ref[...])
    for g in range(groups):
        cols = slice(g * width, (g + 1) * width)
        scaled = (x_ref[:, cols].astype(F32) * over_group(shrink, g, width)).astype(BF16)
        scaled_ref[:, cols] = scaled
        writes = b_ref[:, g * STATE : (g + 1) * STATE]
        halves = over_group(half, g, width)
        rows = slice(g * STATE, (g + 1) * STATE)
        state_ref[rows, :] = halves * (halves * state_ref[rows, :] + dot(writes, scaled, TN))


def scan_kernel(
    scaled_ref, b_ref, c_ref, decay_ref, enter_ref, rows_ref, held_ref, state_ref, *, groups
):
    chunk = pl.program_id(0)
    width = scaled_ref.shape[1] // groups

    @pl.when(chunk == 0)
    def _():
        state_ref[...] = enter_ref[...]

    grow, _, half = chunk_decays(decay_ref[...])
    mask = causal_mask()
    for g in range(groups):
        cols = slice(g * width, (g + 1) * width)
        rows = slice(g * STATE, (g + 1) * STATE)
        scaled = scaled_ref[:, cols]
        writes = b_ref[:, rows]
        reads = c_ref[:, rows]
        halves = over_group(half, g, width)
        held = halves * state_ref[rows, :]
        held_low = held.astype(BF16)
        held_ref[0, rows, :] = held_low
        affinity = jnp.where(mask, dot(reads, writes, NT), 0.0).astype(BF16)
        out = dot(affinity, scaled, NN) + dot(reads, held_low, NN)
        out = out * over_group(grow, g, width)
        rows_ref[cols, :] = out.T.astype(BF16)
        state_ref[rows, :] = halves * (held + dot(writes, scaled, TN))


def pulls_kernel(grad_ref, c_ref, decay_ref, scaled_ref, state_ref, *, groups):
    step = pl.program_id(0)
    width = grad_ref.shape[1] // groups

    @pl.when(step == 0)
    def _():
        state_ref[...] = jnp.zeros_like(state_ref)

    grow, _, half = chunk_decays(decay_ref[...])
    for g in range(groups):
        cols = slice(g * width, (g + 1) * width)
        rows = slice(g * STATE, (g + 1) * STATE)
        scaled = (grad_ref[:, cols].astype(F32) * over_group(grow, g, width)).astype(BF16)
        scaled_ref[:, cols] = scaled
        halves = over_group(half, g, width)
        pulled = dot(c_ref[:, rows], scaled, TN)
        state_ref[rows, :] = halves * (halves * state_ref[rows, :] + pulled)


def grads_kernel(
    grad_ref, scaled_ref, b_ref, c_ref, decay_ref, held_ref, leave_ref,
    x_grad_ref, b_grad_ref, c_grad_ref, state_ref, *, groups,
):
    step = pl.program_id(0)
    width = grad_ref.shape[1] // groups

    @pl.when(step == 0)
    def _():
        state_ref[...] = leave_ref[...]

    _, shrink, half = chunk_decays(decay_ref[...])
    mask = causal_mask()
    for g in range(groups):
        cols = slice(g * width, (g + 1) * width)
        rows = slice(g * STATE, (g + 1) * STATE)
        grad = grad_ref[:, cols]
        scaled = scaled_ref[:, cols]
        writes = b_ref[:, rows]
        reads = c_ref[:, rows]
        halves = over_group(half, g, width)
        left = halves * state_ref[rows, :]
        left_low = left.astype(BF16)
        affinity = jnp.where(mask, dot(reads, writes, NT), 0.0).astype(BF16)
        x_grad = dot(affinity, grad, TN) + dot(writes, left_low, NN)
        x_grad_ref[:, cols] = (x_grad * over_group(shrink, g, width)).astype(BF16)
        pair = jnp.where(mask, dot(grad, scaled, NT), 0.0).astype(BF16)
        c_grad = dot(pair, writes, NN) + dot(grad, held_ref[0, rows, :], NT)
        c_grad_ref[:, rows] = c_grad.astype(BF16)
        b_grad = dot(pair, reads, TN) + dot(scaled, left_low, NT)
        b_grad_ref[:, rows] = b_grad.astype(BF16)
        state_ref[rows, :] = halves * (left + dot(reads, grad, TN))


def scan_calls(tokens, heads, groups):
    inner = heads * HEAD_DIM
    width = inner // groups
    keys = groups * STATE
    chunks = tokens // CHUNK
    call = functools.partial(pl.pallas_call, grid=(chunks,))

    def ahead(cols):
        return pl.BlockSpec((CHUNK, cols), lambda i: (i, 0))

    def back(cols):
        return pl.BlockSpec((CHUNK, cols), lambda i: (chunks - 1 - i, 0))

    decays_ahead = pl.BlockSpec((heads, CHUNK), lambda i: (0, i))
    decays_back = pl.BlockSpec((heads, CHUNK), lambda i: (0, chunks - 1 - i))
    whole = pl.BlockSpec((keys, width), lambda i: (0, 0))
    state_type = jax.ShapeDtypeStruct((keys, width), F32)
    rows_type = jax.ShapeDtypeStruct((tokens, inner), BF16)
    keys_type = jax.ShapeDtypeStruct((tokens, keys), BF16)
    held_type = jax.ShapeDtypeStruct((chunks, keys, width), BF16)
    scratch = [pltpu.VMEM((keys, width), F32)]
    states = call(
        functools.partial(states_kernel, groups=groups),
        in_specs=[ahead(inner), ahead(keys), decays_ahead],
        out_specs=[ahead(inner), whole],
        out_shape=[rows_type, state_type],
        name="states",
    )
    scan = call(
        functools.partial(scan_kernel, groups=groups),
        in_specs=[ahead(inner), ahead(keys), ahead(keys), decays_ahead, whole],
        out_specs=[
            pl.BlockSpec((inner, CHUNK), lambda i: (0, i)),
            pl.BlockSpec((1, keys, width), lambda i: (i, 0, 0)),
        ],
        out_shape=[jax.ShapeDtypeStruct((inner, tokens), BF16), held_type],
        scratch_shapes=scratch,
        name="scan",
    )
    pulls = call(
        functools.partial(pulls_kernel, groups=groups),
        in_specs=[back(inner), back(keys), decays_back],
        out_specs=[back(inner), whole],
        out_shape=[rows_type, state_type],
        name="pulls",
    )
    grads = call(
        functools.partial(grads_kernel, groups=groups),
        in_specs=[
            back(inner), back(inner), back(keys), back(keys), decays_back,
            pl.BlockSpec((1, keys, width), lambda i: (chunks - 1 - i, 0, 0)), whole,
        ],
        out_specs=[back(inner), back(keys), back(keys)],
        out_shape=[rows_type, keys_type, keys_type],
        scratch_shapes=scratch,
        name="grads",
    )
    return states, scan, pulls, grads


def passed_along(shard, axis, by):
    length = lax.axis_size(axis)
    pairs = [(i, i + by) for i in range(length) if 0 <= i + by < length]
    return lax.ppermute(shard, axis, pairs)


def chained(local, log_decay, groups, axis, by):
    incoming = passed_along(local, axis, by)
    turns = lax.axis_size(axis) - 1
    if turns > 1:
        total = jnp.exp(jnp.sum(log_decay, axis=1)).reshape(groups, 1, -1)
        spread = jnp.repeat(total, HEAD_DIM, axis=2)
        spread = jnp.broadcast_to(spread, (groups, STATE, spread.shape[2]))
        spread = spread.reshape(local.shape)

        def turn(_, arrived):
            return passed_along(spread * arrived + local, axis, by)

        incoming = lax.fori_loop(0, turns - 1, turn, incoming)
    return incoming


def any_mesh(rows_t, out_grad, out_weight):
    full = lax.all_gather(out_grad, "tensor", axis=1, tiled=True)
    y_grad = lax.dot_general(
        full, out_weight, (NT, ((), ())), preferred_element_type=F32
    ).astype(BF16)
    part = lax.dot_general(rows_t, full, (NN, ((), ())), preferred_element_type=F32)
    weight_grad = lax.psum_scatter(
        part.astype(BF16), ("dp", "seq"), scatter_dimension=1, tiled=True
    )
    return y_grad, weight_grad


def project_kernel(
    table_ref, zero_ref, one_ref, two_ref, mid_ref, end_ref, rest_ref, near_ref, far_ref, *refs,
    first,
):
    step = pl.program_id(0)
    out_ref, total_ref = refs[-2:]

    def add(own):
        got = dot(own, near_ref[...], NT) + dot(rest_ref[0], far_ref[...], NT)
        return got

    @pl.when(step == 0)
    def _():
        got = add(zero_ref[0])
        total_ref[...] = got if first else refs[0][...] + got

    @pl.when(step == 1)
    def _():
        total_ref[...] += add(one_ref[0])

    @pl.when(step == 2)
    def _():
        total_ref[...] += add(two_ref[0])

    @pl.when(step == 3)
    def _():
        out_ref[...] = (total_ref[...] + add(mid_ref[0] + end_ref[0])).astype(out_ref.dtype)


def project(table, slots, rest, out_weight, part, parts, before):
    tokens, wide = rest.shape[1:]
    inner = out_weight.shape[0]
    first, last = before is None, part == parts - 1
    whole = pl.BlockSpec((tokens, inner), lambda i, t: (0, 0))
    held = pl.BlockSpec((1, tokens, wide), lambda i, t: (0, 0, 0))
    return pl.pallas_call(
        functools.partial(project_kernel, first=first),
        grid_spec=pltpu.PrefetchScalarGridSpec(
            num_scalar_prefetch=1,
            grid=(4,),
            in_specs=[held] * 5
            + [
                pl.BlockSpec((1, tokens, wide), lambda i, t: (i, 0, 0)),
                pl.BlockSpec((inner, wide), lambda i, t: (0, t[4 + i] * parts + part)),
                pl.BlockSpec((inner, wide), lambda i, t: (0, t[8 + i] * parts + part)),
            ]
            + ([] if first else [whole]),
            out_specs=whole,
            scratch_shapes=[pltpu.VMEM((tokens, inner), F32)],
        ),
        out_shape=jax.ShapeDtypeStruct((tokens, inner), BF16 if last else F32),
        name="project",
    )(table, *slots, rest, out_weight, out_weight, *([] if first else [before]))


def partial_kernel(
    table_ref, own_ref, other_ref, zero_ref, one_ref, two_ref, mid_ref, end_ref, *refs, targets,
):
    step = pl.program_id(0)
    half_steps = pl.num_programs(0) // 2
    x_ref, y_ref = refs[:2]
    picked_ref = refs[-1]
    wide = zero_ref.shape[2]

    @pl.when(step == 0)
    def _():
        last = mid_ref[...] + end_ref[...]
        if len(refs) == 4:
            for q, ref in enumerate((zero_ref, one_ref, two_ref)):
                refs[2][q] = ref[1]
            refs[2][3] = last[1]
        for place, target in enumerate(targets):
            cols = slice(place % 2 * wide, (place % 2 + 1) * wide)
            slot = table_ref[target]
            for q, ref in enumerate((zero_ref, one_ref, two_ref)):

                @pl.when(slot == q)
                def _():
                    picked_ref[place // 2, :, :, cols] = ref[...]

            @pl.when(slot == 3)
            def _():
                picked_ref[place // 2, :, :, cols] = last

    def put(side, ref):
        got = dot(own_ref[...], picked_ref[side, 0], NN)
        got += dot(other_ref[...], picked_ref[side, 1], NN)
        got = got.astype(BF16)
        ref[0] = got[:, :wide]
        ref[1] = got[:, wide:]

    @pl.when(step < half_steps)
    def _():
        put(0, x_ref)

    @pl.when(step >= half_steps)
    def _():
        put(1, y_ref)


def partials(table, own, other, slots, targets, with_rest):
    inner, tokens = own.shape
    wide = slots[0].shape[2]
    steps = 4
    tall = inner // steps
    half_steps = steps // 2
    rows = pl.BlockSpec((tall, tokens), lambda i, t: (i, 0))
    held = pl.BlockSpec((2, tokens, wide), lambda i, t: (0, 0, 0))
    out_type = jax.ShapeDtypeStruct((2, inner // 2, wide), BF16)
    out_specs = [
        pl.BlockSpec((2, tall, wide), lambda i, t: (0, jnp.minimum(i, half_steps - 1), 0)),
        pl.BlockSpec((2, tall, wide), lambda i, t: (0, jnp.maximum(i - half_steps, 0), 0)),
    ]
    out_shape = [out_type, out_type]
    if with_rest:
        out_specs.append(pl.BlockSpec((4, tokens, wide), lambda i, t: (0, 0, 0)))
        out_shape.append(jax.ShapeDtypeStruct((4, tokens, wide), BF16))
    return pl.pallas_call(
        functools.partial(partial_kernel, targets=targets),
        grid_spec=pltpu.PrefetchScalarGridSpec(
            num_scalar_prefetch=1,
            grid=(steps,),
            in_specs=[rows, rows] + [held] * 5,
            out_specs=out_specs,
            scratch_shapes=[pltpu.VMEM((2, 2, tokens, 2 * wide), BF16)],
        ),
        out_shape=out_shape,
    )(table, own, other, *slots)


def swapped(value, axis, by):
    return lax.ppermute(value, axis, [(i, i ^ by) for i in range(lax.axis_size(axis))])


def total(*terms):
    return functools.reduce(jnp.add, [t.astype(F32) for t in terms]).astype(BF16)


def after(value, *others):
    return lax.optimization_barrier((value, *others))[0]


def gathered(own, held_up):
    two = swapped(own, "tensor", 2)
    one = swapped(own, "tensor", 1)
    own_late, two_late = own, two
    if held_up:
        own_late, two_late = lax.optimization_barrier((own, two, *held_up))[:2]
    end = lax.ppermute(two_late, "tensor", [(1, 0), (2, 3)])
    mid = lax.ppermute(own_late, "tensor", [(1, 2), (2, 1)])
    return own, one, two, mid, end


def core_halves(out_grad):
    half = out_grad.shape[1] // 2
    core = lax.axis_index("seq")
    mine = lax.dynamic_slice_in_dim(out_grad, core * half, half, 1)
    theirs = lax.dynamic_slice_in_dim(out_grad, (1 - core) * half, half, 1)
    return jnp.stack([mine, swapped(theirs, "seq", 1)])


def this_mesh(rows_t, both, out_weight):
    parts = PARTS
    wide = both.shape[2] // parts
    place = lax.axis_index("tensor")
    repo = lax.axis_index("dp")
    core = lax.axis_index("seq")
    table = jnp.stack(
        [place ^ repo ^ r for r in range(4)]
        + [(place ^ q) * 2 + core for q in range(4)]
        + [(place ^ q) * 2 + 1 - core for q in range(4)]
    ).astype(jnp.int32)
    other = swapped(rows_t, "seq", 1)
    y_grad = None
    pieces = []
    ahead = late = None
    for part in range(parts):
        own = lax.slice_in_dim(both, part * wide, (part + 1) * wide, axis=2)
        if ahead is not None:
            own = after(own, *ahead)
        own, one, two, mid, end = gathered(own, late)
        ahead = (mid, end)
        if part > 0:
            end = after(end, y_grad, x_kept, y_kept)
        slots = own, one, two, mid, end
        x_send, y_send, rest = partials(table, rows_t, other, slots, (1, 3, 2, 3), True)
        late = (x_send,)
        x_got = swapped(x_send, "dp", 1)
        y_got = swapped(y_send, "dp", 2)
        rest = swapped(rest, "seq", 1)
        x_kept, y_kept = partials(table, rows_t, other, slots, (0, 2, 0, 1), False)
        x_last = swapped(total(x_kept[1], x_got[1]), "dp", 2)
        y_last = swapped(total(y_kept[1], y_got[1]), "dp", 1)
        pieces.append(
            jnp.concatenate(
                [total(x_kept[0], x_got[0], x_last), total(y_kept[0], y_got[0], y_last)]
            )
        )
        y_grad = project(table, slots, rest, out_weight, part, parts, y_grad)
    return y_grad, jnp.concatenate(pieces, axis=1)


def per_device(x_in, b_in, c_in, log_decay, out_weight, out_grad):
    x_in, b_in, c_in, log_decay, out_grad = (
        x_in[0], b_in[0], c_in[0], log_decay[0], out_grad[0],
    )
    tokens, heads = log_decay.shape
    log_decay = log_decay.T
    groups = b_in.shape[1] // STATE
    sizes = tuple(lax.axis_size(name) for name in ("dp", "seq", "tensor"))
    here = sizes == THIS_MESH
    if here:
        both = core_halves(out_grad)
        log_decay, both = lax.optimization_barrier((log_decay, both))
    states, scan, pulls, grads = scan_calls(tokens, heads, groups)
    scaled, end_local = states(x_in, b_in, log_decay)
    entering = chained(end_local, log_decay, groups, "seq", 1)
    rows_t, held = scan(scaled, b_in, c_in, log_decay, entering)
    if here:
        y_grad, weight_grad = this_mesh(rows_t, both, out_weight)
    else:
        y_grad, weight_grad = any_mesh(rows_t, out_grad, out_weight)
    grad, start_local = pulls(y_grad, c_in, log_decay)
    leaving = chained(start_local, log_decay, groups, "seq", -1)
    x_grad, b_grad, c_grad = grads(grad, scaled, b_in, c_in, log_decay, held, leaving)
    return weight_grad, x_grad[None], b_grad[None], c_grad[None]


def solution(mesh):
    tokens_spec = P("dp", "seq", "tensor")

    return jax.shard_map(
        per_device,
        mesh=mesh,
        in_specs=(tokens_spec,) * 4 + (P("tensor", None), tokens_spec),
        out_specs=(P("tensor", ("dp", "seq")),) + (tokens_spec,) * 3,
        check_vma=False,
    )
```

```python
import functools

import jax
import jax.numpy as jnp
from jax import lax
from jax.experimental import pallas as pl
from jax.experimental.pallas import tpu as pltpu
from jax.sharding import PartitionSpec as P


HEAD_DIM = 64
STATE = 128
CHUNK = 128
LANES = 128
PER_STEP = 2
FINISH_STEPS = 2
PARTS = 2
THIS_MESH = (4, 2, 4)

BF16 = jnp.bfloat16
F32 = jnp.float32


def dot(a, b, dims):
    return lax.dot_general(a, b, (dims, ((), ())), preferred_element_type=F32)


NN = ((1,), (0,))
NT = ((1,), (1,))
TN = ((0,), (0,))


def causal_mask():
    rows = lax.broadcasted_iota(jnp.int32, (CHUNK, CHUNK), 0)
    cols = lax.broadcasted_iota(jnp.int32, (CHUNK, CHUNK), 1)
    return rows >= cols


def chunk_decays(decays):
    ones = jnp.where(causal_mask(), 1.0, 0.0).astype(BF16)
    first = decays.astype(BF16)
    rest = decays - first.astype(F32)
    second = rest.astype(BF16)
    third = (rest - second.astype(F32)).astype(BF16)
    running = dot(ones, first, NT) + dot(ones, second, NT) + dot(ones, third, NT)
    half = 0.5 * running[CHUNK - 1 : CHUNK, :]
    return jnp.exp(running - half), jnp.exp(half - running), jnp.exp(half)


def over_columns(factors, block):
    rows = factors.shape[0]
    per_block = LANES // HEAD_DIM
    lanes = lax.broadcasted_iota(jnp.int32, (rows, LANES), 1)
    head = block * per_block
    return jnp.where(
        lanes < HEAD_DIM,
        jnp.broadcast_to(factors[:, head : head + 1], (rows, LANES)),
        jnp.broadcast_to(factors[:, head + 1 : head + 2], (rows, LANES)),
    )


def over_group(factors, group, width):
    blocks = width // LANES
    return jnp.concatenate(
        [over_columns(factors, group * blocks + i) for i in range(blocks)], axis=1
    )


def states_kernel(x_ref, b_ref, decay_ref, scaled_ref, state_ref, *, groups):
    width = x_ref.shape[1] // groups

    @pl.when(pl.program_id(0) == 0)
    def _():
        state_ref[...] = jnp.zeros_like(state_ref)

    for c in range(x_ref.shape[0] // CHUNK):
        now = slice(c * CHUNK, (c + 1) * CHUNK)
        _, shrink, half = chunk_decays(decay_ref[:, now])
        for g in range(groups):
            cols = slice(g * width, (g + 1) * width)
            rows = slice(g * STATE, (g + 1) * STATE)
            scaled = (x_ref[now, cols].astype(F32) * over_group(shrink, g, width)).astype(BF16)
            scaled_ref[now, cols] = scaled
            halves = over_group(half, g, width)
            added = dot(b_ref[now, rows], scaled, TN)
            state_ref[rows, :] = halves * (halves * state_ref[rows, :] + added)


def scan_kernel(
    scaled_ref, b_ref, c_ref, decay_ref, enter_ref, rows_ref, held_ref, state_ref, *, groups
):
    width = scaled_ref.shape[1] // groups

    @pl.when(pl.program_id(0) == 0)
    def _():
        state_ref[...] = enter_ref[...]

    mask = causal_mask()
    for c in range(scaled_ref.shape[0] // CHUNK):
        now = slice(c * CHUNK, (c + 1) * CHUNK)
        grow, _, half = chunk_decays(decay_ref[:, now])
        for g in range(groups):
            cols = slice(g * width, (g + 1) * width)
            rows = slice(g * STATE, (g + 1) * STATE)
            scaled = scaled_ref[now, cols]
            writes = b_ref[now, rows]
            reads = c_ref[now, rows]
            halves = over_group(half, g, width)
            held = halves * state_ref[rows, :]
            held_low = held.astype(BF16)
            held_ref[c, rows, :] = held_low
            affinity = jnp.where(mask, dot(reads, writes, NT), 0.0).astype(BF16)
            out = dot(affinity, scaled, NN) + dot(reads, held_low, NN)
            out = out * over_group(grow, g, width)
            rows_ref[cols, now] = out.T.astype(BF16)
            state_ref[rows, :] = halves * (held + dot(writes, scaled, TN))


def pulls_kernel(grad_ref, c_ref, decay_ref, scaled_ref, state_ref, *, groups):
    width = grad_ref.shape[1] // groups

    @pl.when(pl.program_id(0) == 0)
    def _():
        state_ref[...] = jnp.zeros_like(state_ref)

    for c in reversed(range(grad_ref.shape[0] // CHUNK)):
        now = slice(c * CHUNK, (c + 1) * CHUNK)
        grow, _, half = chunk_decays(decay_ref[:, now])
        for g in range(groups):
            cols = slice(g * width, (g + 1) * width)
            rows = slice(g * STATE, (g + 1) * STATE)
            scaled = (grad_ref[now, cols].astype(F32) * over_group(grow, g, width)).astype(BF16)
            scaled_ref[now, cols] = scaled
            halves = over_group(half, g, width)
            pulled = dot(c_ref[now, rows], scaled, TN)
            state_ref[rows, :] = halves * (halves * state_ref[rows, :] + pulled)


def grads_kernel(
    grad_ref, scaled_ref, b_ref, c_ref, decay_ref, held_ref, leave_ref,
    x_grad_ref, b_grad_ref, c_grad_ref, state_ref, *, groups,
):
    width = grad_ref.shape[1] // groups

    @pl.when(pl.program_id(0) == 0)
    def _():
        state_ref[...] = leave_ref[...]

    mask = causal_mask()
    for c in reversed(range(grad_ref.shape[0] // CHUNK)):
        now = slice(c * CHUNK, (c + 1) * CHUNK)
        _, shrink, half = chunk_decays(decay_ref[:, now])
        for g in range(groups):
            cols = slice(g * width, (g + 1) * width)
            rows = slice(g * STATE, (g + 1) * STATE)
            grad = grad_ref[now, cols]
            scaled = scaled_ref[now, cols]
            writes = b_ref[now, rows]
            reads = c_ref[now, rows]
            halves = over_group(half, g, width)
            left = halves * state_ref[rows, :]
            left_low = left.astype(BF16)
            affinity = jnp.where(mask, dot(reads, writes, NT), 0.0).astype(BF16)
            x_grad = dot(affinity, grad, TN) + dot(writes, left_low, NN)
            x_grad_ref[now, cols] = (x_grad * over_group(shrink, g, width)).astype(BF16)
            pair = jnp.where(mask, dot(grad, scaled, NT), 0.0).astype(BF16)
            c_grad = dot(pair, writes, NN) + dot(grad, held_ref[c, rows, :], NT)
            c_grad_ref[now, rows] = c_grad.astype(BF16)
            b_grad = dot(pair, reads, TN) + dot(scaled, left_low, NT)
            b_grad_ref[now, rows] = b_grad.astype(BF16)
            state_ref[rows, :] = halves * (left + dot(reads, grad, TN))


def scan_calls(tokens, heads, groups):
    inner = heads * HEAD_DIM
    width = inner // groups
    keys = groups * STATE
    chunks = tokens // CHUNK
    per_step = PER_STEP if chunks % PER_STEP == 0 else 1
    steps = chunks // per_step
    tall = per_step * CHUNK
    call = functools.partial(pl.pallas_call, grid=(steps,))

    def ahead(cols):
        return pl.BlockSpec((tall, cols), lambda i: (i, 0))

    def back(cols):
        return pl.BlockSpec((tall, cols), lambda i: (steps - 1 - i, 0))

    decays_ahead = pl.BlockSpec((heads, tall), lambda i: (0, i))
    decays_back = pl.BlockSpec((heads, tall), lambda i: (0, steps - 1 - i))
    whole = pl.BlockSpec((keys, width), lambda i: (0, 0))
    state_type = jax.ShapeDtypeStruct((keys, width), F32)
    rows_type = jax.ShapeDtypeStruct((tokens, inner), BF16)
    keys_type = jax.ShapeDtypeStruct((tokens, keys), BF16)
    held_type = jax.ShapeDtypeStruct((chunks, keys, width), BF16)
    scratch = [pltpu.VMEM((keys, width), F32)]
    states = call(
        functools.partial(states_kernel, groups=groups),
        in_specs=[ahead(inner), ahead(keys), decays_ahead],
        out_specs=[ahead(inner), whole],
        out_shape=[rows_type, state_type],
        name="states",
    )
    scan = call(
        functools.partial(scan_kernel, groups=groups),
        in_specs=[ahead(inner), ahead(keys), ahead(keys), decays_ahead, whole],
        out_specs=[
            pl.BlockSpec((inner, tall), lambda i: (0, i)),
            pl.BlockSpec((per_step, keys, width), lambda i: (i, 0, 0)),
        ],
        out_shape=[jax.ShapeDtypeStruct((inner, tokens), BF16), held_type],
        scratch_shapes=scratch,
        name="scan",
    )
    pulls = call(
        functools.partial(pulls_kernel, groups=groups),
        in_specs=[back(inner), back(keys), decays_back],
        out_specs=[back(inner), whole],
        out_shape=[rows_type, state_type],
        name="pulls",
    )
    grads = call(
        functools.partial(grads_kernel, groups=groups),
        in_specs=[
            back(inner), back(inner), back(keys), back(keys), decays_back,
            pl.BlockSpec((per_step, keys, width), lambda i: (steps - 1 - i, 0, 0)), whole,
        ],
        out_specs=[back(inner), back(keys), back(keys)],
        out_shape=[rows_type, keys_type, keys_type],
        scratch_shapes=scratch,
        name="grads",
    )
    return states, scan, pulls, grads


def passed_along(shard, axis, by):
    length = lax.axis_size(axis)
    pairs = [(i, i + by) for i in range(length) if 0 <= i + by < length]
    return lax.ppermute(shard, axis, pairs)


def chained(local, log_decay, groups, axis, by):
    incoming = passed_along(local, axis, by)
    turns = lax.axis_size(axis) - 1
    if turns > 1:
        total = jnp.exp(jnp.sum(log_decay, axis=1)).reshape(groups, 1, -1)
        spread = jnp.repeat(total, HEAD_DIM, axis=2)
        spread = jnp.broadcast_to(spread, (groups, STATE, spread.shape[2]))
        spread = spread.reshape(local.shape)

        def turn(_, arrived):
            return passed_along(spread * arrived + local, axis, by)

        incoming = lax.fori_loop(0, turns - 1, turn, incoming)
    return incoming


def any_mesh(rows_t, out_grad, out_weight):
    full = lax.all_gather(out_grad, "tensor", axis=1, tiled=True)
    y_grad = lax.dot_general(
        full, out_weight, (NT, ((), ())), preferred_element_type=F32
    ).astype(BF16)
    part = lax.dot_general(rows_t, full, (NN, ((), ())), preferred_element_type=F32)
    weight_grad = lax.psum_scatter(
        part.astype(BF16), ("dp", "seq"), scatter_dimension=1, tiled=True
    )
    return y_grad, weight_grad


def project_kernel(table_ref, *refs, blocks, first, flip):
    step = pl.program_id(0)
    low_ref, high_ref = refs[-4:-2]
    out_ref, total_ref = refs[-2:]
    sources = refs[:-4] if first else refs[:-5]
    steps = len(blocks) // 2
    for i in range(steps):

        @pl.when(step == i)
        def _():
            low, high = (pick(sources) for pick in blocks[2 * i : 2 * i + 2])
            got = dot(low_ref[...], low, NT) + dot(high_ref[...], high, NT)
            if i > 0:
                got += total_ref[...]
            elif not first:
                got += refs[-5][...]
            if i < steps - 1:
                total_ref[...] = got
            elif flip:
                out_ref[...] = got.T.astype(out_ref.dtype)
            else:
                out_ref[...] = got


def project(table, at, sources, blocks, out_weight, wide, before, flip):
    tokens = sources[0].shape[-2]
    inner = out_weight.shape[0]
    whole = pl.BlockSpec((inner, tokens), lambda i, t: (0, 0))
    flipped = pl.BlockSpec((tokens, inner), lambda i, t: (0, 0))

    def held(source):
        return pl.BlockSpec(source.shape, lambda i, t: (0,) * source.ndim)

    given = [] if before is None else [before]
    return pl.pallas_call(
        functools.partial(project_kernel, blocks=blocks, first=before is None, flip=flip),
        grid_spec=pltpu.PrefetchScalarGridSpec(
            num_scalar_prefetch=1,
            grid=(len(blocks) // 2,),
            in_specs=[held(source) for source in sources]
            + [whole] * len(given)
            + [
                pl.BlockSpec((inner, wide), lambda i, t: (0, t[at + 2 * i])),
                pl.BlockSpec((inner, wide), lambda i, t: (0, t[at + 2 * i + 1])),
            ],
            out_specs=flipped if flip else whole,
            scratch_shapes=[pltpu.VMEM((inner, tokens), F32)],
        ),
        out_shape=jax.ShapeDtypeStruct(*(((tokens, inner), BF16) if flip else ((inner, tokens), F32))),
        name="project",
    )(table, *sources, *given, out_weight, out_weight)


def partial_kernel(
    table_ref, own_ref, other_ref, zero_ref, one_ref, two_ref, mid_ref, end_ref,
    x_send_ref, y_send_ref, x_keep_ref, y_keep_ref, rest_ref, last_ref, picked_ref,
):
    step = pl.program_id(0)
    half_steps = pl.num_programs(0) // 2
    wide = zero_ref.shape[2]

    @pl.when(step == 0)
    def _():
        last = mid_ref[...] + end_ref[...]
        last_ref[...] = last[0]
        rest_ref[0] = one_ref[1]
        rest_ref[1] = two_ref[1]
        rest_ref[2] = last[1]
        for target in range(4):
            cols = slice(target * wide, (target + 1) * wide)
            slot = table_ref[target]
            for q, ref in enumerate((zero_ref, one_ref, two_ref)):

                @pl.when(slot == q)
                def _():
                    picked_ref[:, :, cols] = ref[...]

            @pl.when(slot == 3)
            def _():
                picked_ref[:, :, cols] = last

    def put(*places):
        for target, (ref, place) in enumerate(places):
            cols = slice(target * wide, (target + 1) * wide)
            got = dot(own_ref[...], picked_ref[0, :, cols], NN)
            got += dot(other_ref[...], picked_ref[1, :, cols], NN)
            ref[place] = got.astype(BF16)

    @pl.when(step < half_steps)
    def _():
        put((x_keep_ref, 0), (x_send_ref, 0), (x_keep_ref, 1), (x_send_ref, 1))

    @pl.when(step >= half_steps)
    def _():
        put((y_keep_ref, 0), (y_keep_ref, 1), (y_send_ref, 0), (y_send_ref, 1))


def partials(table, own, other, slots):
    inner, tokens = own.shape
    wide = slots[0].shape[2]
    steps = 4
    tall = inner // steps
    half_steps = steps // 2
    rows = pl.BlockSpec((tall, tokens), lambda i, t: (i, 0))
    held = pl.BlockSpec((2, tokens, wide), lambda i, t: (0, 0, 0))
    out_type = jax.ShapeDtypeStruct((2, inner // 2, wide), BF16)
    upper = pl.BlockSpec((2, tall, wide), lambda i, t: (0, jnp.minimum(i, half_steps - 1), 0))
    lower = pl.BlockSpec((2, tall, wide), lambda i, t: (0, jnp.maximum(i - half_steps, 0), 0))
    return pl.pallas_call(
        partial_kernel,
        grid_spec=pltpu.PrefetchScalarGridSpec(
            num_scalar_prefetch=1,
            grid=(steps,),
            in_specs=[rows, rows] + [held] * 5,
            out_specs=[
                upper, lower, upper, lower,
                pl.BlockSpec((3, tokens, wide), lambda i, t: (0, 0, 0)),
                pl.BlockSpec((tokens, wide), lambda i, t: (0, 0)),
            ],
            scratch_shapes=[pltpu.VMEM((2, tokens, 4 * wide), BF16)],
        ),
        out_shape=[out_type] * 4
        + [
            jax.ShapeDtypeStruct((3, tokens, wide), BF16),
            jax.ShapeDtypeStruct((tokens, wide), BF16),
        ],
        name="partials",
    )(table, own, other, *slots)


def finish_kernel(x_keep_ref, x_got_ref, x_last_ref, y_keep_ref, y_got_ref, y_last_ref, *refs):
    out_ref = refs[-1]

    def put(place, keep_ref, got_ref, last_ref):
        summed = keep_ref[0].astype(F32) + got_ref[0].astype(F32) + last_ref[...].astype(F32)
        out_ref[place] = summed.astype(BF16)

    put(0, x_keep_ref, x_got_ref, x_last_ref)
    put(1, y_keep_ref, y_got_ref, y_last_ref)


def finish(x_terms, y_terms, part, parts, before):
    half, wide = x_terms[2].shape
    steps = FINISH_STEPS
    tall = half // steps
    specs = [
        pl.BlockSpec((1, tall, wide), lambda i: (0, i, 0)),
        pl.BlockSpec((1, tall, wide), lambda i: (0, i, 0)),
        pl.BlockSpec((tall, wide), lambda i: (i, 0)),
    ]
    given = [] if before is None else [before]
    return pl.pallas_call(
        finish_kernel,
        grid=(steps,),
        in_specs=specs * 2 + [pl.BlockSpec(memory_space=pl.ANY)] * len(given),
        out_specs=pl.BlockSpec((2, tall, wide), lambda i: (0, i, part)),
        out_shape=jax.ShapeDtypeStruct((2, half, parts * wide), BF16),
        input_output_aliases={6: 0} if given else {},
        name="finish",
    )(*x_terms, *y_terms, *given)


def swapped(value, axis, by):
    return lax.ppermute(value, axis, [(i, i ^ by) for i in range(lax.axis_size(axis))])


def total(*terms):
    return functools.reduce(jnp.add, [t.astype(F32) for t in terms]).astype(BF16)


def after(value, *others):
    return lax.optimization_barrier((value, *others))[0]


def gathered(own, held_up):
    two = swapped(own, "tensor", 2)
    one = swapped(own, "tensor", 1)
    own_late, two_late = own, two
    if held_up:
        own_late, two_late = lax.optimization_barrier((own, two, *held_up))[:2]
    end = lax.ppermute(two_late, "tensor", [(1, 0), (2, 3)])
    mid = lax.ppermute(own_late, "tensor", [(1, 2), (2, 1)])
    return own, one, two, mid, end


def core_halves(out_grad):
    half = out_grad.shape[1] // 2
    core = lax.axis_index("seq")
    mine = lax.dynamic_slice_in_dim(out_grad, core * half, half, 1)
    theirs = lax.dynamic_slice_in_dim(out_grad, (1 - core) * half, half, 1)
    return jnp.stack([mine, swapped(theirs, "seq", 1)])


def this_mesh(rows_t, out_grad, both, out_weight):
    parts = PARTS
    wide = both.shape[2] // parts
    place = lax.axis_index("tensor")
    repo = lax.axis_index("dp")
    core = lax.axis_index("seq")

    def column(q, half, part):
        return ((place ^ q) * 2 + half) * parts + part

    mine, rest_half = core, 1 - core
    table = jnp.stack(
        [place ^ repo ^ r for r in range(4)]
        + [place * 4 + i for i in range(4)]
        + [column(q, mine, 0) for q in (1, 2)]
        + [column(q, rest_half, 0) for q in (1, 2, 3)]
        + [column(3, mine, 0)]
        + [column(q, mine, 1) for q in (1, 2, 3)]
        + [column(q, rest_half, 1) for q in (1, 2, 3)]
    ).astype(jnp.int32)
    other = swapped(rows_t, "seq", 1)
    y_grad = weight_grad = None
    ahead = late = None
    for part in range(parts):
        own = lax.slice_in_dim(both, part * wide, (part + 1) * wide, axis=2)
        if ahead is not None:
            own = after(own, *ahead)
        own, one, two, mid, end = gathered(own, late)
        ahead = (mid, end)
        if part == 0:
            blocks = [lambda r, i=i: r[0][:, i * wide : (i + 1) * wide] for i in range(4)]
            blocks += [lambda r: r[1][0], lambda r: r[2][0]]
            y_grad = project(table, 4, (out_grad, one, two), blocks, out_weight, wide, None, False)
        else:
            end = after(end, y_grad)
        x_send, y_send, x_keep, y_keep, rest, last = partials(
            table, rows_t, other, (own, one, two, mid, end)
        )
        late = (x_send,)
        x_got = swapped(x_send, "dp", 1)
        y_got = swapped(y_send, "dp", 2)
        rest = swapped(rest, "seq", 1)
        x_last = swapped(total(x_keep[1], x_got[1]), "dp", 2)
        y_last = swapped(total(y_keep[1], y_got[1]), "dp", 1)
        weight_grad = finish(
            (x_keep, x_got, x_last), (y_keep, y_got, y_last), part, parts, weight_grad
        )
        from_rest = [lambda r, i=i: r[0][i] for i in range(3)]
        if part == 0:
            y_grad = project(
                table, 10, (rest, last), from_rest + [lambda r: r[1][...]],
                out_weight, wide, y_grad, False,
            )
        else:
            blocks = [lambda r: r[1][0], lambda r: r[2][0], lambda r: r[3][...]]
            y_grad = project(
                table, 14, (rest, one, two, last), blocks + from_rest,
                out_weight, wide, y_grad, True,
            )
    return y_grad, weight_grad.reshape(-1, parts * wide)


def per_device(x_in, b_in, c_in, log_decay, out_weight, out_grad):
    x_in, b_in, c_in, log_decay, out_grad = (
        x_in[0], b_in[0], c_in[0], log_decay[0], out_grad[0],
    )
    tokens, heads = log_decay.shape
    log_decay = log_decay.T
    groups = b_in.shape[1] // STATE
    sizes = tuple(lax.axis_size(name) for name in ("dp", "seq", "tensor"))
    here = sizes == THIS_MESH
    if here:
        both = core_halves(out_grad)
        log_decay, both = lax.optimization_barrier((log_decay, both))
    states, scan, pulls, grads = scan_calls(tokens, heads, groups)
    scaled, end_local = states(x_in, b_in, log_decay)
    entering = chained(end_local, log_decay, groups, "seq", 1)
    rows_t, held = scan(scaled, b_in, c_in, log_decay, entering)
    if here:
        y_grad, weight_grad = this_mesh(rows_t, out_grad, both, out_weight)
    else:
        y_grad, weight_grad = any_mesh(rows_t, out_grad, out_weight)
    grad, start_local = pulls(y_grad, c_in, log_decay)
    leaving = chained(start_local, log_decay, groups, "seq", -1)
    x_grad, b_grad, c_grad = grads(grad, scaled, b_in, c_in, log_decay, held, leaving)
    return weight_grad, x_grad[None], b_grad[None], c_grad[None]


def solution(mesh):
    tokens_spec = P("dp", "seq", "tensor")

    program = jax.shard_map(
        per_device,
        mesh=mesh,
        in_specs=(tokens_spec,) * 4 + (P("tensor", None), tokens_spec),
        out_specs=(P("tensor", ("dp", "seq")),) + (tokens_spec,) * 3,
        check_vma=False,
    )
    if tuple(mesh.shape[name] for name in ("dp", "seq", "tensor")) != THIS_MESH:
        return program
    return program
```
